32 devices in a mesh: tok: 16 (over z, x, core), head: 2 (over y).
Axes of the slice: x: 2, y: 2, z: 4, core: 2. Of those that a mesh axis runs over, the one named last changes fastest.
Arguments:
- qkv: bfloat16 [2048, 3, 7168], P(('tok', 'head')), may hold values from -80 to 80
- prefix_cache: bfloat16 [16, 256, 2, 7168], P('tok', None, None, 'head'), may hold values from -80 to 80
- suffix_lengths: int32 [16, 8], P('tok'), may hold values from 1 to 24, 128 in all within a row
- request_groups: int32 [16, 8], P('tok'), may hold values from 0 to 15, all different within a row
- prefix_owner: int32 [16], replicated, may hold values from 0 to 15, each once
Outputs:
- attended: bfloat16 [2048, 7168], P(('tok', 'head'))
- suffix_cache: bfloat16 [2048, 2, 7168], P('tok', None, 'head')
The draws below stay inside these ranges and needn't reach their ends.
Inputs may be any that keep to these rules, and one draw needn't show every extreme that they name: `suffix_lengths`: each row sums to 128; in each row the longest request has exactly 24 tokens. `request_groups`: the 8 requests of one row belong to 8 different groups; every group is read by some request. `prefix_owner`: every slot holds exactly one group.
All inputs are finite; a program needn't handle non-finite values.
Results may differ from the reference program's by a relative error of at most 0.003.
Values may be sent and summed in bfloat16 or wider, within the bound.
A program may use at most 64 MiB of HBM per device.

```python
import math
import jax
import jax.numpy as jnp
import numpy as np
from jax import lax

H = 32
HD = 224
TOK_DEV = 128
PRE = 256
HH = 7168
TOKENS = 2048
G = 16
REQ = 8
CAP = 24
N_TOK = 16


def draw_qkv(key, part):
    keys = jax.random.split(jax.random.fold_in(key, 11), 2)
    noise = jax.random.normal(keys[0], (TOKENS, 3, HH), jnp.float32)
    base = jax.random.normal(keys[1], (TOKENS + 3, HH), jnp.float32)
    nearby = 0.3 * (base[3:] + base[2:-1] + base[1:-2] + base[:-3])
    query = noise[:, 0] + nearby
    keyrows = noise[:, 1] + nearby
    values = noise[:, 2]
    stacked = jnp.stack([query, keyrows, values], axis=1)
    return jnp.clip(stacked, -80.0, 80.0).astype(jnp.bfloat16)


def draw_prefix_cache(key, part):
    keys = jax.random.split(jax.random.fold_in(key, 13), 1)
    cache = jax.random.normal(keys[0], (G, PRE, 2, HH), jnp.float32)
    return jnp.clip(cache, -80.0, 80.0).astype(jnp.bfloat16)


def choose_distinct(key, rows, amount, top, lift):
    ranking = jax.random.permutation(jax.random.fold_in(key, 1), amount)
    pull = ranking
    for power in range(3):
        pull = pull * pull // amount
    pull = pull * lift // amount
    tickets = jax.random.randint(jax.random.fold_in(key, 2), (rows, amount), 0, 4096) + pull
    holders = jax.random.permutation(jax.random.fold_in(key, 3), rows)[jnp.arange(amount) % rows]
    tickets = jnp.where(jnp.arange(rows)[:, None] == holders[None, :], 1 << 14, tickets)
    priority = tickets * amount + jnp.arange(amount)
    return lax.top_k(priority.astype(jnp.int32), top)[1].astype(jnp.int32)


def profile(count, total, most, skew):
    portions = [(1 << 20) // math.isqrt(standing ** skew) + 1 for standing in range(2, count + 1)]
    spare, holding = total - most - (count - 1), [1] * (count - 1)
    while spare > 0:
        free = [i for i in range(count - 1) if holding[i] < most]
        pool, left = sum([portions[i] for i in free]), spare
        for i in free:
            extra = min(most - holding[i], max(1, left * portions[i] // pool), spare)
            holding[i] = holding[i] + extra
            spare = spare - extra
    return np.array([most] + holding)


def uneven(own_key, number_of, total, reach, skew):
    if number_of == 2:
        one = jax.random.randint(own_key, (), max(1, total - reach), min(reach, total - 1) + 1)
        return jnp.stack([one, total - one])
    sizes = jnp.asarray(profile(number_of, total, reach, skew), jnp.int32)
    pairs = (number_of - 1) // 2
    giver, sink = sizes[1:1 + 2 * pairs:2], sizes[2:2 + 2 * pairs:2]
    room = jnp.minimum(giver - 1, reach - sink)
    shifted = jax.random.randint(jax.random.fold_in(own_key, 1), (pairs,), 0, 1 << 20) % (room + 1)
    sizes = sizes.at[1:1 + 2 * pairs:2].set(giver - shifted).at[2:2 + 2 * pairs:2].set(sink + shifted)
    return sizes[jax.random.permutation(jax.random.fold_in(own_key, 2), number_of)]


def setup_inputs(seed: int = 0) -> dict:
    key_of = jax.random.split(jax.random.key(seed), 6)
    return {
        "qkv": draw_qkv(jax.random.fold_in(key_of[5], 71), 0),
        "prefix_cache": draw_prefix_cache(jax.random.fold_in(key_of[5], 71), 0),
        "suffix_lengths": jax.vmap(lambda own: uneven(own, REQ, TOK_DEV, CAP, 2))(jax.random.split(key_of[2], N_TOK)).reshape((N_TOK, REQ)).astype(jnp.int32),
        "request_groups": choose_distinct(key_of[3], N_TOK, G, REQ, 8192),
        "prefix_owner": jax.random.permutation(key_of[4], G).astype(jnp.int32),
    }


def reference(qkv, prefix_cache, suffix_lengths, request_groups, prefix_owner):
    scale = 1.0 / math.sqrt(HD)
    blocks = qkv.reshape(N_TOK, TOK_DEV, 3, H, HD)

    def one_device(args):
        rows, lengths, groups = args
        ends = jnp.cumsum(lengths).astype(jnp.int32)
        starts = (ends - lengths).astype(jnp.int32)
        position = jnp.arange(TOK_DEV, dtype=jnp.int32)
        request = lax.optimization_barrier(jnp.sum((position[:, None] >= ends[None, :]).astype(jnp.int32), axis=1))
        query = rows[:, 0].astype(jnp.float32)
        keyrows = rows[:, 1].astype(jnp.float32)
        values = rows[:, 2]
        scores = jnp.einsum('thd,shd->hts', query, keyrows) * scale
        allowed = (request[:, None] == request[None, :]) & (position[None, :] <= position[:, None])
        scores = jnp.where(allowed[None], scores, -jnp.inf)
        peak_s = lax.optimization_barrier(jnp.max(scores, axis=2))
        weights = jnp.exp(scores - peak_s[:, :, None])
        total_s = lax.optimization_barrier(jnp.sum(weights, axis=2))
        mixed_s = jnp.einsum('hts,shd->thd', weights.astype(jnp.bfloat16).astype(jnp.float32), values.astype(jnp.float32))

        def one_request(index):
            slot = jnp.sum(jnp.where(jnp.arange(G, dtype=jnp.int32) == groups[index], prefix_owner, 0)).astype(jnp.int32)
            cache = lax.dynamic_index_in_dim(prefix_cache, slot, 0, keepdims=False)
            cache_keys = cache[:, 0].reshape(PRE, H, HD).astype(jnp.float32)
            cache_values = cache[:, 1].reshape(PRE, H, HD).astype(jnp.float32)
            picks = jnp.clip(starts[index] + jnp.arange(CAP, dtype=jnp.int32), 0, TOK_DEV - 1)
            chosen = query[picks]
            prefix_scores = jnp.einsum('chd,phd->hcp', chosen, cache_keys) * scale
            peak = lax.optimization_barrier(jnp.max(prefix_scores, axis=2))
            raised = jnp.exp(prefix_scores - peak[:, :, None])
            total = lax.optimization_barrier(jnp.sum(raised, axis=2))
            mixed = jnp.einsum('hcp,phd->chd', raised.astype(jnp.bfloat16).astype(jnp.float32), cache_values)
            mixed = mixed / jnp.transpose(total)[:, :, None]
            return (mixed, jnp.transpose(peak), jnp.transpose(total))
        mixed_p, peak_p, total_p = lax.map(one_request, jnp.arange(REQ, dtype=jnp.int32))
        offset = position - starts[request]
        o_tok = mixed_p[request, offset]
        m_tok = peak_p[request, offset]
        l_tok = total_p[request, offset]
        m_s = jnp.transpose(peak_s)
        l_s = jnp.transpose(total_s)
        top = jnp.maximum(m_tok, m_s)
        first = l_tok * jnp.exp(m_tok - top)
        second = jnp.exp(m_s - top)
        merged = (first[:, :, None] * o_tok + second[:, :, None] * mixed_s) / (first + second * l_s)[:, :, None]
        return merged.reshape(TOK_DEV, HH).astype(jnp.bfloat16)
    attended = lax.map(one_device, (blocks, suffix_lengths, request_groups))
    attended = attended.reshape(TOKENS, HH)
    suffix_cache = qkv[:, 1:3]
    return (attended, suffix_cache)
```

```python
import functools
import math

import jax
import jax.numpy as jnp
from jax import lax
from jax.experimental import pallas as pl
from jax.experimental.pallas import tpu as pltpu
from jax.sharding import PartitionSpec as P

HD = 224
LANES = 128
BAND = math.lcm(HD, LANES)
PER = BAND // HD
LSPLIT = LANES // 2


def window(j):
    low = j * HD // LANES * LANES
    high = -(-(j + 1) * HD // LANES) * LANES
    return low, high


def owners_of(tile):
    first = tile * LANES // HD
    last = ((tile + 1) * LANES - 1) // HD
    return first, last


def lane_iota(shape):
    return lax.broadcasted_iota(jnp.int32, shape, len(shape) - 1)


def by_tile(tile, pick):
    first, last = owners_of(tile)
    left = pick(first)
    if first == last:
        return left
    right = pick(last)
    edge = last * HD - tile * LANES
    return jnp.where(lane_iota((right.shape[0], LANES)) < edge, left, right)


def masked_query(query, j):
    low, high = window(j)
    cols = lane_iota((query.shape[0], high - low)) + low
    keep = (cols >= j * HD) & (cols < (j + 1) * HD)
    return jnp.where(keep, query[:, low:high], jnp.zeros((), query.dtype))


def dot_nt(a, b):
    return lax.dot_general(a, b, (((1,), (1,)), ((), ())), preferred_element_type=jnp.float32)


def dot_nn(a, b):
    return lax.dot_general(a, b, (((1,), (0,)), ((), ())), preferred_element_type=jnp.float32)


def spread_kernel(target_ref, query_ref, out_ref):
    rows = out_ref.shape[0]
    toks = target_ref.shape[1]
    place = lax.broadcasted_iota(jnp.int32, (rows, toks), 0)
    pick = jnp.where(place == target_ref[...], 1.0, 0.0).astype(jnp.bfloat16)
    out_ref[...] = dot_nn(pick, query_ref[...]).astype(jnp.bfloat16)


def attend(query, keys, values, allowed, scale, normalise, put, stats_ref):
    band = pl.program_id(0)
    rows = query.shape[0]
    lanes = lane_iota((rows, LANES))

    @pl.when(band == 0)
    def _():
        stats_ref[...] = jnp.zeros_like(stats_ref)

    stats = stats_ref[...]
    mixed = []
    for j in range(PER):
        low, high = window(j)
        scores = dot_nt(masked_query(query, j), keys[:, low:high]) * scale
        if allowed is not None:
            scores = jnp.where(allowed, scores, -jnp.inf)
        peak = jnp.max(scores, axis=1, keepdims=True)
        raised = jnp.exp(scores - peak)
        total = jnp.sum(raised, axis=1, keepdims=True)
        out = dot_nn(raised.astype(jnp.bfloat16), values[:, low:high])
        if normalise:
            out = out / total
        mixed.append(out)
        head = band * PER + j
        stats = jnp.where(lanes == head, peak, stats)
        stats = jnp.where(lanes == head + LSPLIT, total, stats)
    stats_ref[...] = stats
    for tile in range(BAND // LANES):
        put(tile, by_tile(tile, lambda j: mixed[j][:, tile * LANES - window(j)[0]:][:, :LANES]))


def prefix_kernel(scale, query_ref, key_ref, value_ref, out_ref, stats_ref):
    def put(tile, cols):
        out_ref[:, tile * LANES:(tile + 1) * LANES] = cols.astype(out_ref.dtype)

    attend(query_ref[...], key_ref[...], value_ref[...], None, scale, True, put, stats_ref)


def suffix_kernel(scale, reqc_ref, reqr_ref, query_ref, key_ref, value_ref, out_ref, stats_ref):
    toks = query_ref.shape[0]
    shape = (toks, toks)
    allowed = (reqc_ref[...] == reqr_ref[...]) & (
        lax.broadcasted_iota(jnp.int32, shape, 1) <= lax.broadcasted_iota(jnp.int32, shape, 0)
    )

    def put(tile, cols):
        out_ref[:, tile * LANES:(tile + 1) * LANES] = cols

    keys = key_ref[...].reshape(toks, BAND)
    values = value_ref[...].reshape(toks, BAND)
    attend(query_ref[...], keys, values, allowed, scale, False, put, stats_ref)


def merge_kernel(target_ref, back_ref, pstats_ref, mixed_ref, sstats_ref, out_ref):
    band = pl.program_id(0)
    rows = back_ref.shape[0]
    toks = target_ref.shape[0]
    place = lane_iota((toks, rows))
    pick = jnp.where(place == target_ref[...], 1.0, 0.0).astype(jnp.bfloat16)
    full = pstats_ref[...]
    high = full.astype(jnp.bfloat16)
    rest = full - high.astype(jnp.float32)
    mid = rest.astype(jnp.bfloat16)
    low = (rest - mid.astype(jnp.float32)).astype(jnp.bfloat16)
    prefix = (dot_nn(pick, high) + dot_nn(pick, mid)) + dot_nn(pick, low)
    suffix = sstats_ref[...]
    top = jnp.maximum(prefix, suffix)
    first = pltpu.roll(prefix, LSPLIT, 1) * jnp.exp(prefix - top)
    second = jnp.exp(suffix - top)
    below = first + second * pltpu.roll(suffix, LSPLIT, 1)
    wp = first / below
    ws = second / below
    lanes = lane_iota((toks, LANES))

    def column(weights, j):
        return jnp.sum(jnp.where(lanes == band * PER + j, weights, 0.0), axis=1, keepdims=True)

    cp = [column(wp, j) for j in range(PER)]
    cs = [column(ws, j) for j in range(PER)]
    for tile in range(BAND // LANES):
        cols = slice(tile * LANES, (tile + 1) * LANES)
        back = dot_nn(pick, back_ref[:, cols])
        merged = by_tile(tile, lambda j: cp[j]) * back + by_tile(tile, lambda j: cs[j]) * mixed_ref[:, cols]
        out_ref[:, cols] = merged.astype(out_ref.dtype)


def whole_block(array):
    return pl.BlockSpec(array.shape, lambda g: (0,) * array.ndim)


def band_block(rows):
    return pl.BlockSpec((rows, BAND), lambda g: (0, g))


def cost(flops, moved):
    return pl.CostEstimate(flops=flops, bytes_accessed=moved, transcendentals=0)


def exchange(x, axis):
    return lax.all_to_all(x, axis, split_axis=0, concat_axis=0, tiled=True)


def per_device(qkv, prefix_cache, suffix_lengths, request_groups, prefix_owner):
    n_head = lax.axis_size("head")
    n_tok = lax.axis_size("tok")
    here = qkv.shape[0]
    width = qkv.shape[2] // n_head
    toks = here * n_head
    scale = 1.0 / math.sqrt(HD)
    bands = width // BAND
    capacity = 3 * toks // n_tok
    rows = n_tok * capacity
    planes = jnp.transpose(qkv, (1, 0, 2)).reshape(3, here, n_head, width)
    query = exchange(jnp.transpose(planes[0], (1, 0, 2)), "head").reshape(toks, width)
    kv = exchange(jnp.transpose(planes[1:], (2, 0, 1, 3)), "head")

    lengths = suffix_lengths[0]
    groups = request_groups[0]
    requests = lengths.shape[0]
    ends = jnp.sum(jnp.where(jnp.arange(requests)[:, None] <= jnp.arange(requests)[None, :], lengths[:, None], 0), axis=0)
    starts = ends - lengths
    slots = jnp.sum(jnp.where(groups[:, None] == jnp.arange(n_tok)[None, :], prefix_owner[None, :], 0), axis=1)
    position = jnp.arange(toks, dtype=jnp.int32)
    request = jnp.sum((position[:, None] >= ends[None, :]).astype(jnp.int32), axis=1)
    base = slots * capacity - starts
    inside = request[:, None] == jnp.arange(requests, dtype=jnp.int32)[None, :]
    target = (position + jnp.sum(jnp.where(inside, base[None, :], 0), axis=1)).astype(jnp.int32)
    target_row = target[None, :]
    target_col = target[:, None]

    outgoing = pl.pallas_call(
        spread_kernel,
        grid=(bands,),
        out_shape=jax.ShapeDtypeStruct((rows, width), jnp.bfloat16),
        in_specs=[whole_block(target_row), band_block(toks)],
        out_specs=band_block(rows),
        cost_estimate=cost(2 * rows * toks * width, 2 * (rows + toks) * width),
        name="spread",
    )(target_row, query)
    received = exchange(outgoing.reshape(n_tok, capacity, width), "tok").reshape(rows, width)

    prefix_len = prefix_cache.shape[1]
    cache_keys = prefix_cache[0, :, 0]
    cache_values = prefix_cache[0, :, 1]
    mixed, stats = pl.pallas_call(
        functools.partial(prefix_kernel, scale),
        grid=(bands,),
        out_shape=[
            jax.ShapeDtypeStruct((rows, width), jnp.bfloat16),
            jax.ShapeDtypeStruct((rows, LANES), jnp.float32),
        ],
        in_specs=[band_block(rows), band_block(prefix_len), band_block(prefix_len)],
        out_specs=[band_block(rows), pl.BlockSpec((rows, LANES), lambda g: (0, 0))],
        cost_estimate=cost(4 * rows * prefix_len * width, 4 * (rows + prefix_len) * width),
        name="prefix",
    )(received, cache_keys, cache_values)
    back = exchange(mixed.reshape(n_tok, capacity, width), "tok").reshape(rows, width)
    back_stats = exchange(stats.reshape(n_tok, capacity, LANES), "tok").reshape(rows, LANES)

    reqc, reqr = request[:, None], request[None, :]
    key_spec = pl.BlockSpec((n_head, None, here, BAND), lambda g: (0, 0, 0, g))
    value_spec = pl.BlockSpec((n_head, None, here, BAND), lambda g: (0, 1, 0, g))
    mixed_s, stats_s = pl.pallas_call(
        functools.partial(suffix_kernel, scale),
        grid=(bands,),
        out_shape=[
            jax.ShapeDtypeStruct((toks, width), jnp.float32),
            jax.ShapeDtypeStruct((toks, LANES), jnp.float32),
        ],
        in_specs=[whole_block(reqc), whole_block(reqr), band_block(toks), key_spec, value_spec],
        out_specs=[band_block(toks), pl.BlockSpec((toks, LANES), lambda g: (0, 0))],
        cost_estimate=cost(4 * toks * toks * width, 10 * toks * width),
        name="suffix",
    )(reqc, reqr, query, kv, kv)

    merged = pl.pallas_call(
        merge_kernel,
        grid=(bands,),
        out_shape=jax.ShapeDtypeStruct((toks, width), jnp.bfloat16),
        in_specs=[
            whole_block(target_col),
            band_block(rows),
            whole_block(back_stats),
            band_block(toks),
            whole_block(stats_s),
        ],
        out_specs=band_block(toks),
        cost_estimate=cost(2 * rows * toks * width, 2 * (rows + 3 * toks) * width),
        name="merge",
    )(target_col, back, back_stats, mixed_s, stats_s)
    final = exchange(merged.reshape(n_head, here, width), "head")
    attended = jnp.transpose(final, (1, 0, 2)).reshape(here, n_head * width)
    suffix_cache = jnp.transpose(kv, (0, 2, 1, 3)).reshape(toks, 2, width)
    return (attended, suffix_cache)


def solution(mesh):
    in_specs = (
        P(("tok", "head"), None, None),
        P("tok", None, None, "head"),
        P("tok", None),
        P("tok", None),
        P(),
    )
    out_specs = (P(("tok", "head"), None), P("tok", None, "head"))
    return jax.shard_map(
        per_device, mesh=mesh, in_specs=in_specs, out_specs=out_specs, check_vma=False
    )
```

```python
import functools
import math

import jax
import jax.numpy as jnp
from jax import lax
from jax.experimental import pallas as pl
from jax.experimental.pallas import tpu as pltpu
from jax.sharding import PartitionSpec as P

HD = 224
LANES = 128
BAND = math.lcm(HD, LANES)
PER = BAND // HD
LSPLIT = 16
PIECE = 2 * LSPLIT
PARTS = 2


def window(j):
    low = j * HD // LANES * LANES
    high = -(-(j + 1) * HD // LANES) * LANES
    return low, high


def owners_of(tile):
    first = tile * LANES // HD
    last = ((tile + 1) * LANES - 1) // HD
    return first, last


def lane_iota(shape):
    return lax.broadcasted_iota(jnp.int32, shape, len(shape) - 1)


def by_tile(tile, pick):
    first, last = owners_of(tile)
    left = pick(first)
    if first == last:
        return left
    right = pick(last)
    edge = last * HD - tile * LANES
    return jnp.where(lane_iota((right.shape[0], LANES)) < edge, left, right)


def masked_query(query, j):
    low, high = window(j)
    cols = lane_iota((query.shape[0], high - low)) + low
    keep = (cols >= j * HD) & (cols < (j + 1) * HD)
    return jnp.where(keep, query[:, low:high], jnp.zeros((), query.dtype))


def dot_nt(a, b):
    return lax.dot_general(a, b, (((1,), (1,)), ((), ())), preferred_element_type=jnp.float32)


def dot_nn(a, b):
    return lax.dot_general(a, b, (((1,), (0,)), ((), ())), preferred_element_type=jnp.float32)


def spread_kernel(target_ref, query_ref, out_ref):
    rows = out_ref.shape[0]
    toks = target_ref.shape[1]
    place = lax.broadcasted_iota(jnp.int32, (rows, toks), 0)
    pick = jnp.where(place == target_ref[...], 1.0, 0.0).astype(jnp.bfloat16)
    out_ref[...] = dot_nn(pick, query_ref[...]).astype(jnp.bfloat16)


def attend(query, keys, values, allowed, scale, normalise, put, stats_ref):
    band = pl.program_id(0)
    rows = query.shape[0]
    lanes = lane_iota((rows, LANES))

    @pl.when(band == 0)
    def _():
        stats_ref[...] = jnp.zeros_like(stats_ref)

    stats = stats_ref[...]
    mixed = []
    for j in range(PER):
        low, high = window(j)
        scores = dot_nt(masked_query(query, j), keys[:, low:high]) * scale
        if allowed is not None:
            scores = jnp.where(allowed, scores, -jnp.inf)
        peak = jnp.max(scores, axis=1, keepdims=True)
        raised = jnp.exp(scores - peak)
        total = jnp.sum(raised, axis=1, keepdims=True)
        out = dot_nn(raised.astype(jnp.bfloat16), values[:, low:high])
        if normalise:
            out = out / total
        mixed.append(out)
        head = band * PER + j
        stats = jnp.where(lanes == head, peak, stats)
        stats = jnp.where(lanes == head + LSPLIT, total, stats)
    stats_ref[...] = stats
    for tile in range(BAND // LANES):
        put(tile, by_tile(tile, lambda j: mixed[j][:, tile * LANES - window(j)[0]:][:, :LANES]))


def prefix_kernel(scale, query_ref, key_ref, value_ref, out_ref, stats_ref):
    band = pl.program_id(0)
    bands = pl.num_programs(0)
    width = out_ref.shape[1] - LANES

    def put(tile, cols):
        at = pl.multiple_of(band * BAND + tile * LANES, LANES)
        out_ref[:, pl.ds(at, LANES)] = cols.astype(out_ref.dtype)

    attend(query_ref[...], key_ref[...], value_ref[...], None, scale, True, put, stats_ref)

    @pl.when(band == bands - 1)
    def _():
        full = stats_ref[...]
        high = full.astype(jnp.bfloat16).astype(jnp.float32)
        rest = full - high
        mid = rest.astype(jnp.bfloat16).astype(jnp.float32)
        low = rest - mid
        packed = high + pltpu.roll(mid, PIECE, 1) + pltpu.roll(low, 2 * PIECE, 1)
        out_ref[:, width:] = packed.astype(out_ref.dtype)


def suffix_kernel(scale, reqc_ref, reqr_ref, query_ref, key_ref, value_ref, out_ref, stats_ref):
    toks = query_ref.shape[0]
    shape = (toks, toks)
    allowed = (reqc_ref[...] == reqr_ref[...]) & (
        lax.broadcasted_iota(jnp.int32, shape, 1) <= lax.broadcasted_iota(jnp.int32, shape, 0)
    )

    def put(tile, cols):
        out_ref[:, tile * LANES:(tile + 1) * LANES] = cols

    keys = key_ref[...].reshape(toks, BAND)
    values = value_ref[...].reshape(toks, BAND)
    attend(query_ref[...], keys, values, allowed, scale, False, put, stats_ref)


def merge_kernel(target_ref, back_ref, pstats_ref, mixed_ref, sstats_ref, out_ref):
    band = pl.program_id(0)
    rows = back_ref.shape[0]
    toks = target_ref.shape[0]
    place = lane_iota((toks, rows))
    pick = jnp.where(place == target_ref[...], 1.0, 0.0).astype(jnp.bfloat16)
    packed = dot_nn(pick, pstats_ref[...])
    prefix = (packed + pltpu.roll(packed, LANES - PIECE, 1)) + pltpu.roll(
        packed, LANES - 2 * PIECE, 1
    )
    suffix = sstats_ref[...]
    top = jnp.maximum(prefix, suffix)
    first = pltpu.roll(prefix, LANES - LSPLIT, 1) * jnp.exp(prefix - top)
    second = jnp.exp(suffix - top)
    below = first + second * pltpu.roll(suffix, LANES - LSPLIT, 1)
    wp = first / below
    ws = second / below
    lanes = lane_iota((toks, LANES))

    def column(weights, j):
        return jnp.sum(jnp.where(lanes == band * PER + j, weights, 0.0), axis=1, keepdims=True)

    cp = [column(wp, j) for j in range(PER)]
    cs = [column(ws, j) for j in range(PER)]
    for tile in range(BAND // LANES):
        cols = slice(tile * LANES, (tile + 1) * LANES)
        back = dot_nn(pick, back_ref[:, cols])
        merged = by_tile(tile, lambda j: cp[j]) * back + by_tile(tile, lambda j: cs[j]) * mixed_ref[:, cols]
        out_ref[:, cols] = merged.astype(out_ref.dtype)


def whole_block(array):
    return pl.BlockSpec(array.shape, lambda g: (0,) * array.ndim)


def band_block(rows, off=0):
    return pl.BlockSpec((rows, BAND), lambda g: (0, g + off))


def cost(flops, moved):
    return pl.CostEstimate(flops=flops, bytes_accessed=moved, transcendentals=0)


def exchange(x, axis):
    return lax.all_to_all(x, axis, split_axis=0, concat_axis=0, tiled=True)


def shift_exchange(x, axis):
    n = lax.axis_size(axis)
    me = lax.axis_index(axis)
    parts = [lax.dynamic_index_in_dim(x, me, 0, keepdims=False)]
    for d in range(1, n):
        ring = [(i, (i + d) % n) for i in range(n)]
        sent = lax.dynamic_index_in_dim(x, lax.rem(me + d, n), 0, keepdims=False)
        parts.append(lax.ppermute(sent, axis, ring))
    out = []
    for source in range(n):
        picked = parts[0]
        for d in range(1, n):
            picked = jnp.where(lax.rem(me + n - source, n) == d, parts[d], picked)
        out.append(picked)
    return jnp.stack(out)


def per_device(qkv, prefix_cache, suffix_lengths, request_groups, prefix_owner):
    n_head = lax.axis_size("head")
    n_tok = lax.axis_size("tok")
    here = qkv.shape[0]
    width = qkv.shape[2] // n_head
    toks = here * n_head
    scale = 1.0 / math.sqrt(HD)
    bands = width // BAND
    parts = PARTS if bands % PARTS == 0 else 1
    each = bands // parts
    cols = each * BAND
    capacity = 3 * toks // n_tok
    rows = n_tok * capacity
    planes = jnp.transpose(qkv, (1, 0, 2)).reshape(3, here, n_head, width)
    queries = [
        exchange(jnp.transpose(planes[0, :, :, p * cols:(p + 1) * cols], (1, 0, 2)), "head").reshape(toks, cols)
        for p in range(parts)
    ]
    kv_send = jnp.transpose(planes[1:], (2, 0, 1, 3))

    lengths = suffix_lengths[0]
    groups = request_groups[0]
    requests = lengths.shape[0]
    ends = jnp.sum(jnp.where(jnp.arange(requests)[:, None] <= jnp.arange(requests)[None, :], lengths[:, None], 0), axis=0)
    starts = ends - lengths
    slots = jnp.sum(jnp.where(groups[:, None] == jnp.arange(n_tok)[None, :], prefix_owner[None, :], 0), axis=1)
    position = jnp.arange(toks, dtype=jnp.int32)
    request = jnp.sum((position[:, None] >= ends[None, :]).astype(jnp.int32), axis=1)
    base = slots * capacity - starts
    inside = request[:, None] == jnp.arange(requests, dtype=jnp.int32)[None, :]
    target = (position + jnp.sum(jnp.where(inside, base[None, :], 0), axis=1)).astype(jnp.int32)
    target_row = target[None, :]
    target_col = target[:, None]
    reqc, reqr = request[:, None], request[None, :]

    prefix_len = prefix_cache.shape[1]
    queries[0], cache_keys, cache_values = lax.optimization_barrier(
        (queries[0], prefix_cache[0, :, 0], prefix_cache[0, :, 1])
    )
    received = []
    for p in range(parts):
        outgoing = pl.pallas_call(
            spread_kernel,
            grid=(each,),
            out_shape=jax.ShapeDtypeStruct((rows, cols), jnp.bfloat16),
            in_specs=[whole_block(target_row), band_block(toks)],
            out_specs=band_block(rows),
            cost_estimate=cost(2 * rows * toks * cols, 2 * (rows + toks) * cols),
            name="spread",
        )(target_row, queries[p])
        if p == 0:
            outgoing, kv_send = lax.optimization_barrier((outgoing, kv_send))
        received.append(exchange(outgoing.reshape(n_tok, capacity, cols), "tok").reshape(rows, cols))
    kv = shift_exchange(kv_send, "head")
    received[-1], kv = lax.optimization_barrier((received[-1], kv))

    back = []
    for p in range(parts):
        mixed = pl.pallas_call(
            functools.partial(prefix_kernel, scale),
            grid=(each,),
            out_shape=jax.ShapeDtypeStruct((rows, cols + LANES), jnp.bfloat16),
            in_specs=[band_block(rows), band_block(prefix_len, p * each), band_block(prefix_len, p * each)],
            out_specs=pl.BlockSpec((rows, cols + LANES), lambda g: (0, 0)),
            scratch_shapes=[pltpu.VMEM((rows, LANES), jnp.float32)],
            cost_estimate=cost(4 * rows * prefix_len * cols, 4 * (rows + prefix_len) * cols),
            name="prefix",
        )(received[p], cache_keys, cache_values)
        back.append(exchange(mixed.reshape(n_tok, capacity, cols + LANES), "tok").reshape(rows, cols + LANES))

    finals = []
    for p in range(parts):
        key_spec = pl.BlockSpec((n_head, None, here, BAND), lambda g, p=p: (0, 0, 0, g + p * each))
        value_spec = pl.BlockSpec((n_head, None, here, BAND), lambda g, p=p: (0, 1, 0, g + p * each))
        mixed_s, stats_s = pl.pallas_call(
            functools.partial(suffix_kernel, scale),
            grid=(each,),
            out_shape=[
                jax.ShapeDtypeStruct((toks, cols), jnp.float32),
                jax.ShapeDtypeStruct((toks, LANES), jnp.float32),
            ],
            in_specs=[whole_block(reqc), whole_block(reqr), band_block(toks), key_spec, value_spec],
            out_specs=[band_block(toks), pl.BlockSpec((toks, LANES), lambda g: (0, 0))],
            cost_estimate=cost(4 * toks * toks * cols, 10 * toks * cols),
            name="suffix",
        )(reqc, reqr, queries[p], kv, kv)
        merged = pl.pallas_call(
            merge_kernel,
            grid=(each,),
            out_shape=jax.ShapeDtypeStruct((toks, cols), jnp.bfloat16),
            in_specs=[
                whole_block(target_col),
                band_block(rows),
                pl.BlockSpec((rows, LANES), lambda g: (0, cols // LANES)),
                band_block(toks),
                whole_block(stats_s),
            ],
            out_specs=band_block(toks),
            cost_estimate=cost(2 * rows * toks * cols, 2 * (rows + 3 * toks) * cols),
            name="merge",
        )(target_col, back[p], back[p], mixed_s, stats_s)
        finals.append(exchange(merged.reshape(n_head, here, cols), "head"))
    attended = jnp.transpose(jnp.stack(finals, axis=2), (1, 0, 2, 3)).reshape(here, n_head * width)
    suffix_cache = jnp.transpose(kv, (0, 2, 1, 3)).reshape(toks, 2, width)
    return (attended, suffix_cache)


def solution(mesh):
    in_specs = (
        P(("tok", "head"), None, None),
        P("tok", None, None, "head"),
        P("tok", None),
        P("tok", None),
        P(),
    )
    out_specs = (P(("tok", "head"), None), P("tok", None, "head"))
    return jax.shard_map(
        per_device, mesh=mesh, in_specs=in_specs, out_specs=out_specs, check_vma=False
    )
```
